128 devices in a mesh: req: 32 (over y, z, core), head: 4 (over x).
Axes of the slice: x: 4, y: 4, z: 4, core: 2. Of those that a mesh axis runs over, the one named last changes fastest.
Arguments:
- queries: bfloat16 [64, 512, 4096], P('req', None, 'head'), may hold values from -16 to 16
- new_keys: bfloat16 [64, 512, 1024], P('req', None, 'head'), may hold values from -16 to 16
- incoming_values: bfloat16 [64, 512, 1024], P('req', None, 'head'), may hold values from -6 to 6
- request_cached_keys: bfloat16 [64, 2048, 1024], P('req', None, 'head'), may hold values from -12 to 12
- request_cached_values: bfloat16 [64, 2048, 1024], P('req', None, 'head'), may hold values from -6 to 6
- cache_lengths: int32 [64], P('req'), may hold values from 1 to 2048, 65536 in all
- out_weight: bfloat16 [4096, 4096], P('head'), may hold values from -0.25 to 0.25
- residual: bfloat16 [512, 64, 4096], P(('req', 'head')), may hold values from -3 to 3
- norm_gain: bfloat16 [4096], replicated, may hold values from 0.5 to 1.5
Outputs:
- hidden: bfloat16 [512, 64, 4096], P(('req', 'head'))
- normed: bfloat16 [512, 64, 4096], P(('req', 'head'))
The draws below stay inside these ranges and needn't reach their ends.
Inputs may be any that keep to these rules, and one draw needn't show every extreme that they name: Request r's cache holds keys in slots 0 to cache_lengths[r] - 1; in every draw the longest request has exactly 2048.
All inputs are finite; a program needn't handle non-finite values. No bound on the sum of `cache_lengths` on one device may be relied on, other than what follows from the above.
Results may differ from the reference program's by a relative error of at most 0.013.
Values may be sent and summed in bfloat16 or wider, within the bound.
A program may use at most 128 MiB of HBM per device.

```python
import math
import jax
import jax.numpy as jnp
import numpy as np
from jax import lax

D = 4096
QUERY_HEADS = 32
KEY_VALUE_HEADS = 8
HEAD_SIZE = 128
NEW_TOKEN_COUNT = 512
CACHE_SLOTS = 2048
REQUEST_TOTAL = 64
N_HEAD = 4


def draw_queries(key, part):
    gaussian_sample = jax.random.normal(jax.random.fold_in(key, 1), (REQUEST_TOTAL, NEW_TOKEN_COUNT, QUERY_HEADS * HEAD_SIZE), jnp.float32)
    gaussian_sample = jnp.clip(gaussian_sample, -6.0, 6.0)
    return gaussian_sample.astype(jnp.bfloat16)


def draw_new_keys(key, part):
    gaussian_sample = 2.0 * jax.random.normal(jax.random.fold_in(key, 2), (REQUEST_TOTAL, NEW_TOKEN_COUNT, KEY_VALUE_HEADS * HEAD_SIZE), jnp.float32)
    gaussian_sample = jnp.clip(gaussian_sample, -12.0, 12.0)
    return gaussian_sample.astype(jnp.bfloat16)


def shard_levels(rng, shape, pieces, low, top_value):
    def one(dim, shards_of):
        heights = jax.random.uniform(jax.random.fold_in(jax.random.fold_in(rng, 6), dim), (shards_of,), jnp.float32, low / len(pieces), top_value / len(pieces))
        return jnp.repeat(jnp.exp(heights), shape[dim] // shards_of).reshape((-1,) + (1,) * (len(shape) - dim - 1))

    level = one(*pieces[0])
    for cut in pieces[1:]:
        level = level * one(*cut)
    return level


def profile(amount, total, most, slope):
    portions = [(1 << 20) // math.isqrt(rank ** slope) + 1 for rank in range(2, amount + 1)]
    rest, counts = total - most - (amount - 1), [1] * (amount - 1)
    while rest > 0:
        movable = [i for i in range(amount - 1) if counts[i] < most]
        whole, budget = sum([portions[i] for i in movable]), rest
        for i in movable:
            extra = min(most - counts[i], max(1, budget * portions[i] // whole), rest)
            counts[i] = counts[i] + extra
            rest = rest - extra
    return np.array([most] + counts)


def uneven_parts(key, count, total, limit, skew):
    if count == 2:
        one = jax.random.randint(key, (), max(1, total - limit), min(limit, total - 1) + 1)
        return jnp.stack([one, total - one])
    sizes = jnp.asarray(profile(count, total, limit, skew), jnp.int32)
    couples = (count - 1) // 2
    giver, receiver = sizes[1:1 + 2 * couples:2], sizes[2:2 + 2 * couples:2]
    slack = jnp.minimum(giver - 1, limit - receiver)
    shifted = jax.random.randint(jax.random.fold_in(key, 1), (couples,), 0, 1 << 20) % (slack + 1)
    sizes = sizes.at[1:1 + 2 * couples:2].set(giver - shifted).at[2:2 + 2 * couples:2].set(receiver + shifted)
    return sizes[jax.random.permutation(jax.random.fold_in(key, 2), count)]


def centred(own_key, shape, spread, most, split=(), kind=jnp.bfloat16):
    values = spread * jax.random.normal(own_key, shape, jnp.float32)
    if split:
        values = values * shard_levels(own_key, shape, split, -0.22, 0.18)
    return jnp.clip(values, -most, most).astype(kind)


def setup_inputs(seed: int = 0) -> dict:
    splits = jax.random.split(jax.random.key(seed), 10)
    queries = draw_queries(jax.random.fold_in(splits[9], 71), 0)
    new_keys = draw_new_keys(jax.random.fold_in(splits[9], 71), 0)
    incoming_values = centred(splits[2], (REQUEST_TOTAL, NEW_TOKEN_COUNT, KEY_VALUE_HEADS * HEAD_SIZE), 1.0, 6.0, ((0, 32), (2, 4)))
    request_cached_keys = centred(splits[3], (REQUEST_TOTAL, CACHE_SLOTS, KEY_VALUE_HEADS * HEAD_SIZE), 2.0, 12.0, ((0, 32), (2, 4)))
    request_cached_values = centred(splits[4], (REQUEST_TOTAL, CACHE_SLOTS, KEY_VALUE_HEADS * HEAD_SIZE), 1.0, 6.0, ((0, 32), (2, 4)))
    cache_lengths = uneven_parts(splits[5], REQUEST_TOTAL, REQUEST_TOTAL * CACHE_SLOTS // 2, CACHE_SLOTS, 2).astype(jnp.int32)
    out_weight = centred(splits[6], (QUERY_HEADS * HEAD_SIZE, D), (QUERY_HEADS * HEAD_SIZE // 8) ** -0.5, 0.25, ((0, 4),))
    residual = centred(splits[7], (NEW_TOKEN_COUNT, REQUEST_TOTAL, D), 0.5, 3.0, ((0, 128),))
    norm_gain = jnp.clip(1.0 + 0.1 * jax.random.normal(splits[8], (D,), jnp.float32), 0.5, 1.5).astype(jnp.bfloat16)
    return dict(queries=queries, new_keys=new_keys, incoming_values=incoming_values, request_cached_keys=request_cached_keys, request_cached_values=request_cached_values, cache_lengths=cache_lengths, out_weight=out_weight, residual=residual, norm_gain=norm_gain)


NEGATIVE_FILLER = -1e+30

def soak_into(carried_along, query_head_count, key_row_block, value_row_block, visible, logit_scale):
    running_max, running_sum, running_out = carried_along
    scores = jnp.einsum('qgjd,kgd->gjqk', query_head_count.astype(jnp.float32), key_row_block.astype(jnp.float32)) * logit_scale
    scores = jnp.where(visible, scores, NEGATIVE_FILLER)
    new_max = jnp.maximum(running_max, lax.optimization_barrier(jnp.max(scores, axis=-1)))
    rescale = jnp.exp(running_max - new_max)
    weights = jnp.exp(scores - new_max[..., None])
    running_sum = running_sum * rescale + lax.optimization_barrier(jnp.sum(weights, axis=-1))
    rounded = lax.optimization_barrier(weights.astype(jnp.bfloat16)).astype(jnp.float32)
    running_out = running_out * rescale[..., None] + jnp.einsum('gjqk,kgd->gjqd', rounded, value_row_block.astype(jnp.float32))
    return (new_max, running_sum, running_out)

def attend_one(query_row_block, incoming_key, incoming_value, stored_key_cache, stored_value_cache, length):
    group_members = QUERY_HEADS // KEY_VALUE_HEADS
    query_head_count = query_row_block.reshape(NEW_TOKEN_COUNT, KEY_VALUE_HEADS, group_members, HEAD_SIZE)
    logit_scale = 1.0 / math.sqrt(HEAD_SIZE)
    block_extent = min(512, CACHE_SLOTS)
    carried_along = (jnp.full((KEY_VALUE_HEADS, group_members, NEW_TOKEN_COUNT), NEGATIVE_FILLER, jnp.float32), jnp.zeros((KEY_VALUE_HEADS, group_members, NEW_TOKEN_COUNT), jnp.float32), jnp.zeros((KEY_VALUE_HEADS, group_members, NEW_TOKEN_COUNT, HEAD_SIZE), jnp.float32))
    block_count = (length + block_extent - 1) // block_extent

    def cache_step(block_id, carried_along):
        start_shift = (block_id * block_extent).astype(jnp.int32)
        key_row_block = lax.dynamic_slice_in_dim(stored_key_cache, start_shift, block_extent, 0).reshape(block_extent, KEY_VALUE_HEADS, HEAD_SIZE)
        value_row_block = lax.dynamic_slice_in_dim(stored_value_cache, start_shift, block_extent, 0).reshape(block_extent, KEY_VALUE_HEADS, HEAD_SIZE)
        positions = start_shift + jnp.arange(block_extent, dtype=jnp.int32)
        visible = (positions < length)[None, None, None, :]
        return soak_into(carried_along, query_head_count, key_row_block, value_row_block, visible, logit_scale)
    carried_along = lax.fori_loop(0, block_count, cache_step, carried_along)
    row_index = jnp.arange(NEW_TOKEN_COUNT, dtype=jnp.int32)
    causal_mask = (row_index[None, :] <= row_index[:, None])[None, None, :, :]
    carried_along = soak_into(carried_along, query_head_count, incoming_key.reshape(NEW_TOKEN_COUNT, KEY_VALUE_HEADS, HEAD_SIZE), incoming_value.reshape(NEW_TOKEN_COUNT, KEY_VALUE_HEADS, HEAD_SIZE), causal_mask, logit_scale)
    running_max, running_sum, running_out = carried_along
    finished = running_out / running_sum[..., None]
    return finished.transpose(2, 0, 1, 3).reshape(NEW_TOKEN_COUNT, QUERY_HEADS * HEAD_SIZE).astype(jnp.bfloat16)

def reference(queries, new_keys, incoming_values, request_cached_keys, request_cached_values, cache_lengths, out_weight, residual, norm_gain):
    attended = lax.map(lambda packed: attend_one(*packed), (queries, new_keys, incoming_values, request_cached_keys, request_cached_values, cache_lengths))
    flat_rows = attended.reshape(REQUEST_TOTAL * NEW_TOKEN_COUNT, QUERY_HEADS * HEAD_SIZE)
    group_width = QUERY_HEADS * HEAD_SIZE // N_HEAD
    accumulated = jnp.zeros((REQUEST_TOTAL * NEW_TOKEN_COUNT, D), jnp.float32)
    for group_id in range(N_HEAD):
        partial_term = jnp.dot(flat_rows[:, group_id * group_width:(group_id + 1) * group_width], out_weight[group_id * group_width:(group_id + 1) * group_width], preferred_element_type=jnp.float32)
        accumulated = accumulated + lax.optimization_barrier(partial_term.astype(jnp.bfloat16)).astype(jnp.float32)
    attn_out = accumulated.astype(jnp.bfloat16).reshape(REQUEST_TOTAL, NEW_TOKEN_COUNT, D).transpose(1, 0, 2)
    summed = residual.astype(jnp.float32) + lax.optimization_barrier(attn_out).astype(jnp.float32)
    hidden = summed.astype(jnp.bfloat16)
    mean_square = lax.optimization_barrier(jnp.mean(summed * summed, axis=-1, keepdims=True))
    normed = (summed * lax.rsqrt(mean_square + 1e-05) * norm_gain.astype(jnp.float32)).astype(jnp.bfloat16)
    return (hidden, normed)
```

```python
import math

import jax
import jax.numpy as jnp
from jax import lax
from jax.experimental import pallas as pl
from jax.experimental.pallas import tpu as pltpu
from jax.sharding import PartitionSpec as P

HEAD_SIZE = 128


NEGATIVE_FILLER = -1e30
Q_TILE = 512
K_BLOCK = 512
LOG2_SCALE = math.log2(math.e) / math.sqrt(HEAD_SIZE)
BF16, F32 = jnp.bfloat16, jnp.float32


def attention_kernel(length_ref, q_ref, new_k_ref, new_v_ref, key_ref, value_ref, out_ref, values):
    length = length_ref[pl.program_id(0)]
    slots, span = key_ref.shape[1], new_k_ref.shape[1]
    values[:slots, :HEAD_SIZE] = value_ref[0]
    values[slots:, :HEAD_SIZE] = new_v_ref[0]
    values[:, HEAD_SIZE:] = jnp.ones((slots + span, HEAD_SIZE), BF16)
    contract_last = (((1,), (1,)), ((), ()))

    def one_head(start, member):
        columns = pl.ds(pl.multiple_of(member * HEAD_SIZE, HEAD_SIZE), HEAD_SIZE)
        query = q_ref[0, pl.ds(start, Q_TILE), columns]
        blocks = [(True, at, K_BLOCK) for at in range(0, slots, K_BLOCK)]
        blocks.append((False, 0, start + Q_TILE))
        running_max = total = None
        for cached, at, count in blocks:
            keys = key_ref[0, at : at + count] if cached else new_k_ref[0, :count]
            scores = lax.dot_general(query, keys, contract_last, preferred_element_type=F32)
            if cached:
                slot = lax.broadcasted_iota(jnp.int32, (1, count), 1) + at
                scores = scores + jnp.where(slot < length, 0.0, NEGATIVE_FILLER)
            else:
                row = lax.broadcasted_iota(jnp.int32, (Q_TILE, count), 0) + start
                column = lax.broadcasted_iota(jnp.int32, (Q_TILE, count), 1)
                scores = jnp.where(column <= row, scores, NEGATIVE_FILLER)
            block_max = jnp.max(scores, axis=1, keepdims=True)
            new_max = block_max if total is None else jnp.maximum(running_max, block_max)
            weights = jnp.exp2((scores - new_max) * LOG2_SCALE).astype(BF16)
            rows = values[at : at + count] if cached else values[slots : slots + count]
            product = jnp.dot(weights, rows, preferred_element_type=F32)
            if total is None:
                total = product
            else:
                total = total * jnp.exp2((running_max - new_max) * LOG2_SCALE) + product
            running_max = new_max
        attended = total[:, :HEAD_SIZE] / total[:, HEAD_SIZE:]
        out_ref[0, pl.ds(start, Q_TILE), columns] = attended.astype(BF16)

    for start in range(0, span, Q_TILE):

        def two_heads(pair, carried):
            one_head(start, 2 * pair)
            one_head(start, 2 * pair + 1)
            return carried

        lax.fori_loop(0, q_ref.shape[2] // HEAD_SIZE // 2, two_heads, 0)


def attend(queries, new_keys, new_values, cached_keys, cached_values, lengths):
    requests, span, width = queries.shape
    slots = cached_keys.shape[1]
    key_heads = new_keys.shape[2] // HEAD_SIZE
    group_width = width // key_heads

    def block(rows, columns):
        return pl.BlockSpec((1, rows, columns), lambda r, g, _: (r, 0, g))

    return pl.pallas_call(
        attention_kernel,
        grid_spec=pltpu.PrefetchScalarGridSpec(
            num_scalar_prefetch=1,
            grid=(requests, key_heads),
            in_specs=[
                block(span, group_width),
                block(span, HEAD_SIZE),
                block(span, HEAD_SIZE),
                block(slots, HEAD_SIZE),
                block(slots, HEAD_SIZE),
            ],
            out_specs=block(span, group_width),
            scratch_shapes=[pltpu.VMEM((slots + span, 2 * HEAD_SIZE), BF16)],
        ),
        out_shape=jax.ShapeDtypeStruct(queries.shape, BF16),
        compiler_params=pltpu.CompilerParams(vmem_limit_bytes=60 << 20),
    )(lengths, queries, new_keys, new_values, cached_keys, cached_values)


def row_product(flat_rows, out_weight):
    return jnp.dot(flat_rows, out_weight, preferred_element_type=jnp.float32)


def body(
    queries,
    new_keys,
    incoming_values,
    request_cached_keys,
    request_cached_values,
    cache_lengths,
    out_weight,
    residual,
    norm_gain,
):
    req_local, span_len, query_width = queries.shape
    attended = attend(
        queries,
        new_keys,
        incoming_values,
        request_cached_keys,
        request_cached_values,
        cache_lengths,
    )
    req_count = lax.axis_size("req")
    head_count = lax.axis_size("head")
    piece_len = span_len // (req_count * head_count)
    share_rows = req_count * piece_len * req_local
    arranged = attended.reshape(req_local, req_count, head_count, piece_len, query_width).transpose(
        2, 1, 3, 0, 4
    )
    flat_rows = arranged.reshape(head_count * share_rows, query_width)
    summed = lax.psum_scatter(
        row_product(flat_rows, out_weight).astype(jnp.bfloat16),
        "head",
        scatter_dimension=0,
        tiled=True,
    )
    exchanged = lax.all_to_all(
        summed.reshape(req_count, piece_len, req_local, -1),
        "req",
        split_axis=0,
        concat_axis=2,
        tiled=True,
    )
    attn_rows = exchanged.reshape(piece_len, req_count * req_local, -1)
    summed_rows = residual.astype(jnp.float32) + lax.optimization_barrier(attn_rows).astype(
        jnp.float32
    )
    hidden = summed_rows.astype(jnp.bfloat16)
    mean_square = jnp.mean(summed_rows * summed_rows, axis=-1, keepdims=True)
    normed = (summed_rows * lax.rsqrt(mean_square + 1e-05) * norm_gain.astype(jnp.float32)).astype(
        jnp.bfloat16
    )
    return (hidden, normed)


def solution(mesh):
    placed = (
        P("req", None, "head"),
        P("req", None, "head"),
        P("req", None, "head"),
        P("req", None, "head"),
        P("req", None, "head"),
        P("req"),
        P("head", None),
        P(("req", "head"), None, None),
        P(),
    )
    return jax.shard_map(
        body,
        mesh=mesh,
        in_specs=placed,
        out_specs=(P(("req", "head"), None, None), P(("req", "head"), None, None)),
        check_vma=False,
    )
```

```python
import functools
import math

import jax
import jax.numpy as jnp
from jax import lax
from jax.experimental import pallas as pl
from jax.experimental.pallas import tpu as pltpu
from jax.sharding import PartitionSpec as P

HEAD_SIZE = 128
NEGATIVE_FILLER = -1e30
K_BLOCK = 512
N_TILE = 512
LOG2_SCALE = math.log2(math.e) / math.sqrt(HEAD_SIZE)
BF16, F32 = jnp.bfloat16, jnp.float32
MESH = pl.DeviceIdType.MESH


def spread_kernel(
    sizes,
    length_ref,
    q_hbm,
    new_k_hbm,
    new_v_hbm,
    key_hbm,
    value_hbm,
    weight_hbm,
    gathered,
    query,
    new_keys,
    keys,
    values,
    weight,
    attended,
    rows_of_owner,
    part,
    far_in,
    near_in,
    summed,
    load_sem,
    far_send,
    far_recv,
    near_send,
    near_recv,
    out_send,
    out_recv,
    self_sem,
):
    req_count, head_count, requests, key_heads, members = sizes
    row = lax.axis_index("req")
    me = lax.axis_index("head")
    right = lax.rem(me + 1, head_count)
    left = lax.rem(me + head_count - 1, head_count)
    opposite = lax.rem(me + 2, head_count)
    chunks = part.shape[0]
    slots, span = key_hbm.shape[1], new_k_hbm.shape[1]
    width = weight.shape[1]
    half = width // 2
    lane_groups = [pl.ds(g * HEAD_SIZE, HEAD_SIZE) for g in range(key_heads)]

    barrier = pltpu.get_barrier_semaphore()
    for neighbour in (left, right):
        pl.semaphore_signal(barrier, inc=1, device_id=(row, neighbour), device_id_type=MESH)

    def greet(step, carried):
        peer = lax.rem(row + step, req_count)
        pl.semaphore_signal(barrier, inc=1, device_id=(peer, me), device_id_type=MESH)
        return carried

    lax.fori_loop(1, req_count, greet, 0)

    for r in range(requests):
        for g in range(key_heads):
            values[r, g, :, HEAD_SIZE:] = jnp.ones((slots + span, HEAD_SIZE), BF16)

    loads = []

    def load(source, target):
        copy = pltpu.make_async_copy(source, target, load_sem.at[len(loads)])
        copy.start()
        loads.append(copy)

    for r in range(requests):
        load(q_hbm.at[r], query.at[r])
        load(key_hbm.at[r], keys.at[r])
        load(new_k_hbm.at[r], new_keys.at[r])
        for g, lanes in enumerate(lane_groups):
            load(value_hbm.at[r, :, lanes], values.at[r, g, pl.ds(0, slots), pl.ds(0, HEAD_SIZE)])
            load(new_v_hbm.at[r, :, lanes], values.at[r, g, pl.ds(slots, span), pl.ds(0, HEAD_SIZE)])
    load(weight_hbm, weight)
    per_request = (len(loads) - 1) // requests

    contract_last = (((1,), (1,)), ((), ()))

    def attend(turn, r):
        length = length_ref[r]
        tile = query.shape[1] * 16
        stacked = members * tile
        for g in range(key_heads):
            block = query[r, :, pl.ds(pl.multiple_of(turn * 16, 16), 16), pl.ds(g * members * HEAD_SIZE, members * HEAD_SIZE)]
            block = block.reshape(tile, members * HEAD_SIZE)
            q = jnp.concatenate(
                [block[:, j * HEAD_SIZE : (j + 1) * HEAD_SIZE] for j in range(members)], axis=0
            )
            running_max = total = None
            for at in range(0, slots + span, K_BLOCK):
                cached = at < slots
                if cached:
                    k = keys[r, at : at + K_BLOCK, g * HEAD_SIZE : (g + 1) * HEAD_SIZE]
                else:
                    k = new_keys[r, at - slots : at - slots + K_BLOCK, g * HEAD_SIZE : (g + 1) * HEAD_SIZE]
                scores = lax.dot_general(q, k, contract_last, preferred_element_type=F32)
                if cached:
                    slot = lax.broadcasted_iota(jnp.int32, (1, K_BLOCK), 1) + at
                    scores = scores + jnp.where(slot < length, 0.0, NEGATIVE_FILLER)
                else:
                    line = lax.broadcasted_iota(jnp.int32, (stacked, K_BLOCK), 0)
                    position = ((line >> 4) & 7) * 64 + (line & 15) + turn * 16
                    column = lax.broadcasted_iota(jnp.int32, (stacked, K_BLOCK), 1) + (at - slots)
                    scores = jnp.where(column <= position, scores, NEGATIVE_FILLER)
                block_max = jnp.max(scores, axis=1, keepdims=True)
                new_max = block_max if total is None else jnp.maximum(running_max, block_max)
                weights = jnp.exp2((scores - new_max) * LOG2_SCALE).astype(BF16)
                product = jnp.dot(weights, values[r, g, at : at + K_BLOCK], preferred_element_type=F32)
                if total is None:
                    total = product
                else:
                    total = total * jnp.exp2((running_max - new_max) * LOG2_SCALE) + product
                running_max = new_max
            out = total[:, :HEAD_SIZE] / total[:, HEAD_SIZE:]
            for j in range(members):
                at = (g * members + j) * HEAD_SIZE
                attended[r, :, at : at + HEAD_SIZE] = out[j * tile : (j + 1) * tile]

    def order_rows():
        count = attended.shape[1] // 8
        shape = (count, 8, attended.shape[2])
        first, second = attended[0].reshape(shape), attended[1].reshape(shape)
        upper = lax.broadcasted_iota(jnp.int32, shape, 1) < 4
        even = jnp.where(upper, first, pltpu.roll(second, 4, 1))
        odd = jnp.where(upper, pltpu.roll(first, 4, 1), second)
        for low, rows in enumerate((even, odd)):
            split = rows.reshape(count // 2, 2, 8, shape[2])
            for high in range(2):
                owner = 2 * high + low
                lines = split[:, high].reshape(count * 4, shape[2]).astype(BF16)
                rows_of_owner[owner * count * 4 : (owner + 1) * count * 4] = lines

    def project(c, first):
        def tile(n, carried):
            columns = pl.ds(pl.multiple_of(n * N_TILE, N_TILE), N_TILE)
            product = jnp.dot(rows_of_owner[...], weight[:, columns], preferred_element_type=F32)
            part[c, :, :, columns] = product.astype(BF16).reshape(head_count, -1, N_TILE)
            return carried

        tiles = half // N_TILE
        lax.fori_loop(first * tiles, (first + 1) * tiles, tile, 0)

    def far(c, side):
        return pltpu.make_async_remote_copy(
            src_ref=part.at[c, opposite, :, pl.ds(side * half, half)],
            dst_ref=far_in.at[c, side],
            send_sem=far_send.at[c, side],
            recv_sem=far_recv.at[c, side],
            device_id=(row, (right, left)[side]),
            device_id_type=MESH,
        )

    def near(c, side):
        target = (right, left)[side]
        return pltpu.make_async_remote_copy(
            src_ref=part.at[c, target],
            dst_ref=near_in.at[c, side],
            send_sem=near_send.at[c, side],
            recv_sem=near_recv.at[c, side],
            device_id=(row, target),
            device_id_type=MESH,
        )

    def pass_on(c):
        for side, target in enumerate((right, left)):
            far(c, side).wait_recv()
            columns = pl.ds(side * half, half)
            own = part[c, target, :, columns].astype(F32)
            part[c, target, :, columns] = (own + far_in[c, side].astype(F32)).astype(BF16)
            near(c, side).start()

    group, place = row // chunks, lax.rem(row, chunks)
    groups = req_count // chunks

    def finish(c):
        for side in range(2):
            near(c, side).wait_recv()
        total = part[c, me].astype(F32) + near_in[c, 0].astype(F32) + near_in[c, 1].astype(F32)
        summed[c] = total.reshape(summed.shape[1:]).astype(BF16)

        def send(step, carried):
            outgoing(c, step).start()
            return carried

        if c == 0:
            keep().start()
        lax.fori_loop(1 if c == 0 else 0, groups, send, 0)

    def outgoing(c, step):
        block = lax.rem(group + step, groups)
        target = block * chunks + lax.rem(place + c, chunks)
        return pltpu.make_async_remote_copy(
            src_ref=summed.at[c, block],
            dst_ref=gathered.at[pl.ds(pl.multiple_of(row * 8, 8), 8)],
            send_sem=out_send.at[c, step],
            recv_sem=out_recv.at[row],
            device_id=(target, me),
            device_id_type=MESH,
        )

    def keep():
        lines = gathered.at[pl.ds(pl.multiple_of(row * 8, 8), 8)]
        return pltpu.make_async_copy(summed.at[0, group], lines, self_sem)

    for c in range(chunks):
        turn = lax.rem(place + c, chunks)
        for r in range(requests):
            if c == 0:
                for copy in loads[r * per_request : (r + 1) * per_request]:
                    copy.wait()
            attend(turn, r)
            if c > 0 and r == 0:
                pass_on(c - 1)
        if c > 1:
            finish(c - 2)
        order_rows()
        if c == 0:
            loads[-1].wait()
            pl.semaphore_wait(barrier, 2 + req_count - 1)
        for side in range(2):
            project(c, side)
            far(c, side).start()
    pass_on(chunks - 1)
    for c in range(max(0, chunks - 2), chunks):
        finish(c)

    keep().wait()
    for c in range(chunks):
        for side in range(2):
            far(c, side).wait_send()
            near(c, side).wait_send()

        def sent(step, carried, c=c):
            outgoing(c, step).wait_send()
            return carried

        lax.fori_loop(1 if c == 0 else 0, groups, sent, 0)

    def arrived(step, carried):
        source = lax.rem(row + step, req_count)
        lines = gathered.at[pl.ds(pl.multiple_of(source * 8, 8), 8)]
        pltpu.make_async_remote_copy(
            src_ref=summed.at[0, 0],
            dst_ref=lines,
            send_sem=out_send.at[0, 0],
            recv_sem=out_recv.at[source],
            device_id=(source, me),
            device_id_type=MESH,
        ).wait_recv()
        return carried

    lax.fori_loop(1, req_count, arrived, 0)


def spread(queries, new_keys, new_values, cached_keys, cached_values, lengths, weight):
    requests, span, q_width = queries.shape
    slots, kv_width = cached_keys.shape[1:]
    key_heads = kv_width // HEAD_SIZE
    members = q_width // kv_width
    width = weight.shape[1]
    req_count, head_count = lax.axis_size("req"), lax.axis_size("head")
    chunks = 4
    blocks = req_count // chunks
    tile = blocks * 16
    lines = blocks * 8
    loads = requests * (3 + 2 * key_heads) + 1
    anywhere = pl.BlockSpec(memory_space=pl.ANY)
    dma = pltpu.SemaphoreType.DMA
    return pl.pallas_call(
        functools.partial(spread_kernel, (req_count, head_count, requests, key_heads, members)),
        in_specs=[pl.BlockSpec(memory_space=pltpu.SMEM)] + [anywhere] * 6,
        out_specs=anywhere,
        out_shape=jax.ShapeDtypeStruct((req_count * 8, width), BF16),
        scratch_shapes=[
            pltpu.VMEM((requests, blocks, span // blocks, q_width), BF16),
            pltpu.VMEM((requests, span, kv_width), BF16),
            pltpu.VMEM((requests, slots, kv_width), BF16),
            pltpu.VMEM((requests, key_heads, slots + span, 2 * HEAD_SIZE), BF16),
            pltpu.VMEM(weight.shape, BF16),
            pltpu.VMEM((requests, tile, q_width), F32),
            pltpu.VMEM((requests * tile, q_width), BF16),
            pltpu.VMEM((chunks, head_count, lines, width), BF16),
            pltpu.VMEM((chunks, 2, lines, width // 2), BF16),
            pltpu.VMEM((chunks, 2, lines, width), BF16),
            pltpu.VMEM((chunks, blocks, 8, width), BF16),
            dma((loads,)),
            dma((chunks, 2)),
            dma((chunks, 2)),
            dma((chunks, 2)),
            dma((chunks, 2)),
            dma((chunks, blocks)),
            dma((req_count,)),
            dma,
        ],
        compiler_params=pltpu.CompilerParams(
            collective_id=0, has_side_effects=True, vmem_limit_bytes=63 << 20
        ),
    )(
        lengths,
        queries.reshape(requests, blocks, span // blocks, q_width),
        new_keys,
        new_values,
        cached_keys,
        cached_values,
        weight,
    )


def norm_kernel(rows_ref, residual_ref, gain_ref, hidden_ref, normed_ref):
    count = rows_ref.shape[0]
    positions = residual_ref.shape[0]
    lines = residual_ref.shape[1]
    target = lax.broadcasted_iota(jnp.int32, (count, count), 0)
    source = lax.broadcasted_iota(jnp.int32, (count, count), 1)
    wanted = (target & (lines - 1)) * positions + (target >> 3)
    pick = (source == wanted).astype(F32).astype(BF16)
    moved = jnp.dot(pick, rows_ref[...], preferred_element_type=F32)
    summed = residual_ref[...].astype(F32) + moved.reshape(residual_ref.shape)
    hidden_ref[...] = summed.astype(BF16)
    mean_square = jnp.mean(summed * summed, axis=-1, keepdims=True)
    scale = lax.rsqrt(mean_square + 1e-05)
    normed_ref[...] = (summed * scale * gain_ref[...].astype(F32)).astype(BF16)


def body(
    queries,
    new_keys,
    incoming_values,
    request_cached_keys,
    request_cached_values,
    cache_lengths,
    out_weight,
    residual,
    norm_gain,
):
    gathered = spread(
        queries,
        new_keys,
        incoming_values,
        request_cached_keys,
        request_cached_values,
        cache_lengths,
        out_weight,
    )
    positions, requests, width = residual.shape
    lines = 8
    block = pl.BlockSpec((positions, lines, width), lambda i: (0, i, 0))
    out = jax.ShapeDtypeStruct(residual.shape, BF16)
    hidden, normed = pl.pallas_call(
        norm_kernel,
        grid=(requests // lines,),
        in_specs=[
            pl.BlockSpec((positions * lines, width), lambda i: (i, 0)),
            block,
            pl.BlockSpec((1, 1, width), lambda i: (0, 0, 0)),
        ],
        out_specs=[block, block],
        out_shape=[out, out],
        compiler_params=pltpu.CompilerParams(vmem_limit_bytes=40 << 20),
    )(gathered, residual, norm_gain.reshape(1, 1, width))
    return hidden, normed


def solution(mesh):
    placed = (
        P("req", None, "head"),
        P("req", None, "head"),
        P("req", None, "head"),
        P("req", None, "head"),
        P("req", None, "head"),
        P("req"),
        P("head", None),
        P(("req", "head"), None, None),
        P(),
    )
    return jax.shard_map(
        body,
        mesh=mesh,
        in_specs=placed,
        out_specs=(P(("req", "head"), None, None), P(("req", "head"), None, None)),
        check_vma=False,
    )
```

```python
import functools
import math

import jax
import jax.numpy as jnp
from jax import lax
from jax.experimental import pallas as pl
from jax.experimental.pallas import tpu as pltpu
from jax.sharding import PartitionSpec as P

HEAD_SIZE = 128
NEGATIVE_FILLER = -1e30
K_BLOCK = 512
N_TILE = 512
LOG2_SCALE = math.log2(math.e) / math.sqrt(HEAD_SIZE)
BF16, F32 = jnp.bfloat16, jnp.float32
MESH = pl.DeviceIdType.MESH


def spread_kernel(
    sizes,
    length_ref,
    q_hbm,
    new_k_hbm,
    new_v_hbm,
    key_hbm,
    value_hbm,
    weight_hbm,
    gathered,
    query,
    new_keys,
    keys,
    values,
    weight,
    attended,
    rows_of_owner,
    part,
    far_in,
    near_in,
    summed,
    load_sem,
    weight_sem,
    far_send,
    far_recv,
    near_send,
    near_recv,
    out_send,
    out_recv,
    self_sem,
):
    req_count, head_count, requests, key_heads, members = sizes
    row = lax.axis_index("req")
    me = lax.axis_index("head")
    right = lax.rem(me + 1, head_count)
    left = lax.rem(me + head_count - 1, head_count)
    opposite = lax.rem(me + 2, head_count)
    chunks = part.shape[0]
    slots, span = key_hbm.shape[1], new_k_hbm.shape[1]
    width = weight.shape[1]
    half = width // 2
    lane_groups = [pl.ds(g * HEAD_SIZE, HEAD_SIZE) for g in range(key_heads)]

    barrier = pltpu.get_barrier_semaphore()
    for neighbour in (left, right):
        pl.semaphore_signal(barrier, inc=1, device_id=(row, neighbour), device_id_type=MESH)

    def greet(step, carried):
        peer = lax.rem(row + step, req_count)
        pl.semaphore_signal(barrier, inc=1, device_id=(peer, me), device_id_type=MESH)
        return carried

    lax.fori_loop(1, req_count, greet, 0)

    for r in range(requests):
        for g in range(key_heads):
            values[r, g, :, HEAD_SIZE:] = jnp.ones((slots + span, HEAD_SIZE), BF16)

    def loads(r):
        pairs = [
            (q_hbm.at[r], query.at[r]),
            (key_hbm.at[r], keys.at[r]),
            (new_k_hbm.at[r], new_keys.at[r]),
        ]
        for g, lanes in enumerate(lane_groups):
            old = values.at[r, g, pl.ds(0, slots), pl.ds(0, HEAD_SIZE)]
            new = values.at[r, g, pl.ds(slots, span), pl.ds(0, HEAD_SIZE)]
            pairs += [(value_hbm.at[r, :, lanes], old), (new_v_hbm.at[r, :, lanes], new)]
        return [
            pltpu.make_async_copy(source, target, load_sem.at[r, i])
            for i, (source, target) in enumerate(pairs)
        ]

    for r in range(requests):
        for copy in loads(r):
            copy.start()
    weight_load = pltpu.make_async_copy(weight_hbm, weight, weight_sem)
    weight_load.start()

    contract_last = (((1,), (1,)), ((), ()))

    def attend(turn, r):
        length = length_ref[r]
        tile = query.shape[1] * 16
        stacked = members * tile
        for g in range(key_heads):
            lanes = pl.ds(g * members * HEAD_SIZE, members * HEAD_SIZE)
            rows = query[r, :, pl.ds(pl.multiple_of(turn * 16, 16), 16), lanes]
            rows = rows.reshape(tile, members * HEAD_SIZE)
            q = jnp.concatenate(
                [rows[:, j * HEAD_SIZE : (j + 1) * HEAD_SIZE] for j in range(members)], axis=0
            )
            running_max = total = None
            for at in range(0, slots + span, K_BLOCK):
                cached = at < slots
                if cached:
                    k = keys[r, at : at + K_BLOCK, g * HEAD_SIZE : (g + 1) * HEAD_SIZE]
                else:
                    k = new_keys[r, at - slots : at - slots + K_BLOCK, g * HEAD_SIZE : (g + 1) * HEAD_SIZE]
                scores = lax.dot_general(q, k, contract_last, preferred_element_type=F32)
                if cached:
                    slot = lax.broadcasted_iota(jnp.int32, (1, K_BLOCK), 1) + at
                    scores = scores + jnp.where(slot < length, 0.0, NEGATIVE_FILLER)
                else:
                    line = lax.broadcasted_iota(jnp.int32, (stacked, K_BLOCK), 0)
                    block = (line >> 4) & (query.shape[1] - 1)
                    position = block * query.shape[2] + (line & 15) + turn * 16
                    column = lax.broadcasted_iota(jnp.int32, (stacked, K_BLOCK), 1) + (at - slots)
                    scores = jnp.where(column <= position, scores, NEGATIVE_FILLER)
                block_max = jnp.max(scores, axis=1, keepdims=True)
                new_max = block_max if total is None else jnp.maximum(running_max, block_max)
                weights = jnp.exp2((scores - new_max) * LOG2_SCALE).astype(BF16)
                product = jnp.dot(weights, values[r, g, at : at + K_BLOCK], preferred_element_type=F32)
                if total is None:
                    total = product
                else:
                    total = total * jnp.exp2((running_max - new_max) * LOG2_SCALE) + product
                running_max = new_max
            out = total[:, :HEAD_SIZE] / total[:, HEAD_SIZE:]
            for j in range(members):
                at = (g * members + j) * HEAD_SIZE
                attended[r, :, at : at + HEAD_SIZE] = out[j * tile : (j + 1) * tile]

    def order_rows():
        count = attended.shape[1] // 8
        shape = (count, 8, attended.shape[2])
        first, second = attended[0].reshape(shape), attended[1].reshape(shape)
        upper = lax.broadcasted_iota(jnp.int32, shape, 1) < 4
        even = jnp.where(upper, first, pltpu.roll(second, 4, 1))
        odd = jnp.where(upper, pltpu.roll(first, 4, 1), second)
        for low, rows in enumerate((even, odd)):
            split = rows.reshape(count // 2, 2, 8, shape[2])
            for high in range(2):
                owner = 2 * high + low
                lines = split[:, high].reshape(count * 4, shape[2]).astype(BF16)
                rows_of_owner[owner * count * 4 : (owner + 1) * count * 4] = lines

    def project(c, first):
        def tile(n, carried):
            columns = pl.ds(pl.multiple_of(n * N_TILE, N_TILE), N_TILE)
            product = jnp.dot(rows_of_owner[...], weight[:, columns], preferred_element_type=F32)
            part[c, :, :, columns] = product.astype(BF16).reshape(head_count, -1, N_TILE)
            return carried

        tiles = half // N_TILE
        lax.fori_loop(first * tiles, (first + 1) * tiles, tile, 0)

    def far(c, side):
        return pltpu.make_async_remote_copy(
            src_ref=part.at[c, opposite, :, pl.ds(side * half, half)],
            dst_ref=far_in.at[c, side],
            send_sem=far_send.at[c, side],
            recv_sem=far_recv.at[c, side],
            device_id=(row, (right, left)[side]),
            device_id_type=MESH,
        )

    def near(c, side, summed_half):
        target = (right, left)[side]
        columns = pl.ds((side if summed_half else 1 - side) * half, half)
        return pltpu.make_async_remote_copy(
            src_ref=part.at[c, target, :, columns],
            dst_ref=near_in.at[c, side, :, columns],
            send_sem=near_send.at[c, side, int(summed_half)],
            recv_sem=near_recv.at[c, side, int(summed_half)],
            device_id=(row, target),
            device_id_type=MESH,
        )

    def pass_on(c):
        for side, target in enumerate((right, left)):
            far(c, side).wait_recv()
            columns = pl.ds(side * half, half)
            own = part[c, target, :, columns].astype(F32)
            part[c, target, :, columns] = (own + far_in[c, side].astype(F32)).astype(BF16)
            near(c, side, True).start()

    group, place = row // chunks, lax.rem(row, chunks)
    groups = req_count // chunks

    def finish(c, kept=False):
        for side in range(2):
            near(c, side, False).wait_recv()
            near(c, side, True).wait_recv()
        total = part[c, me].astype(F32) + near_in[c, 0].astype(F32) + near_in[c, 1].astype(F32)
        summed[c] = total.reshape(summed.shape[1:]).astype(BF16)

        def send(step, carried):
            outgoing(c, step).start()
            return carried

        if kept:
            keep().start()
        lax.fori_loop(1 if kept else 0, groups, send, 0)

    def outgoing(c, step):
        block = lax.rem(group + step, groups)
        target = block * chunks + lax.rem(place + c, chunks)
        return pltpu.make_async_remote_copy(
            src_ref=summed.at[c, block],
            dst_ref=gathered.at[pl.ds(pl.multiple_of(row * 8, 8), 8)],
            send_sem=out_send.at[c, step],
            recv_sem=out_recv.at[row],
            device_id=(target, me),
            device_id_type=MESH,
        )

    def keep():
        lines = gathered.at[pl.ds(pl.multiple_of(row * 8, 8), 8)]
        return pltpu.make_async_copy(summed.at[0, group], lines, self_sem)

    def half_chunk(step, carried):
        c, r = lax.div(step, requests), lax.rem(step, requests)

        @pl.when(c == 0)
        def _():
            for copy in loads(r):
                copy.wait()

        @pl.when(step == 1)
        def _():
            pl.semaphore_wait(barrier, 2 + req_count - 1)

        attend(lax.rem(place + c, chunks), r)

        @pl.when(r == requests - 1)
        def _():
            pl.when(c > 0)(lambda: pass_on(c - 1))
            order_rows()

            @pl.when(c == 0)
            def _():
                weight_load.wait()

            for side in range(2):
                project(c, side)
                far(c, side).start()
            for side in range(2):
                near(c, side, False).start()
            pl.when(c == 2)(lambda: finish(0, True))
            pl.when(c > 2)(lambda: finish(c - 2))

        return carried

    lax.fori_loop(0, chunks * requests, half_chunk, 0)
    finish(chunks - 2)
    pass_on(chunks - 1)
    finish(chunks - 1)

    keep().wait()
    for c in range(chunks):
        for side in range(2):
            far(c, side).wait_send()
            near(c, side, False).wait_send()
            near(c, side, True).wait_send()

        def sent(step, carried, c=c):
            outgoing(c, step).wait_send()
            return carried

        lax.fori_loop(1 if c == 0 else 0, groups, sent, 0)

    def arrived(step, carried):
        source = lax.rem(row + step, req_count)
        lines = gathered.at[pl.ds(pl.multiple_of(source * 8, 8), 8)]
        pltpu.make_async_remote_copy(
            src_ref=summed.at[0, 0],
            dst_ref=lines,
            send_sem=out_send.at[0, 0],
            recv_sem=out_recv.at[source],
            device_id=(source, me),
            device_id_type=MESH,
        ).wait_recv()
        return carried

    lax.fori_loop(1, req_count, arrived, 0)


def spread(queries, new_keys, new_values, cached_keys, cached_values, lengths, weight):
    requests, span, q_width = queries.shape
    slots, kv_width = cached_keys.shape[1:]
    key_heads = kv_width // HEAD_SIZE
    members = q_width // kv_width
    width = weight.shape[1]
    req_count, head_count = lax.axis_size("req"), lax.axis_size("head")
    chunks = 8
    blocks = req_count // chunks
    tile = blocks * 16
    lines = blocks * 8
    anywhere = pl.BlockSpec(memory_space=pl.ANY)
    dma = pltpu.SemaphoreType.DMA
    return pl.pallas_call(
        functools.partial(spread_kernel, (req_count, head_count, requests, key_heads, members)),
        in_specs=[pl.BlockSpec(memory_space=pltpu.SMEM)] + [anywhere] * 6,
        out_specs=anywhere,
        out_shape=jax.ShapeDtypeStruct((req_count * 8, width), BF16),
        scratch_shapes=[
            pltpu.VMEM((requests, blocks, span // blocks, q_width), BF16),
            pltpu.VMEM((requests, span, kv_width), BF16),
            pltpu.VMEM((requests, slots, kv_width), BF16),
            pltpu.VMEM((requests, key_heads, slots + span, 2 * HEAD_SIZE), BF16),
            pltpu.VMEM(weight.shape, BF16),
            pltpu.VMEM((requests, tile, q_width), F32),
            pltpu.VMEM((requests * tile, q_width), BF16),
            pltpu.VMEM((chunks, head_count, lines, width), BF16),
            pltpu.VMEM((chunks, 2, lines, width // 2), BF16),
            pltpu.VMEM((chunks, 2, lines, width), BF16),
            pltpu.VMEM((chunks, blocks, 8, width), BF16),
            dma((requests, 3 + 2 * key_heads)),
            dma,
            dma((chunks, 2)),
            dma((chunks, 2)),
            dma((chunks, 2, 2)),
            dma((chunks, 2, 2)),
            dma((chunks, blocks)),
            dma((req_count,)),
            dma,
        ],
        compiler_params=pltpu.CompilerParams(
            collective_id=0, has_side_effects=True, vmem_limit_bytes=63 << 20
        ),
    )(
        lengths,
        queries.reshape(requests, blocks, span // blocks, q_width),
        new_keys,
        new_values,
        cached_keys,
        cached_values,
        weight,
    )


def norm_kernel(rows_ref, residual_ref, gain_ref, hidden_ref, normed_ref):
    count = rows_ref.shape[0]
    positions = residual_ref.shape[0]
    lines = residual_ref.shape[1]
    target = lax.broadcasted_iota(jnp.int32, (count, count), 0)
    source = lax.broadcasted_iota(jnp.int32, (count, count), 1)
    wanted = (target & (lines - 1)) * positions + (target >> (lines.bit_length() - 1))
    pick = (source == wanted).astype(F32).astype(BF16)
    moved = jnp.dot(pick, rows_ref[...], preferred_element_type=F32)
    summed = residual_ref[...].astype(F32) + moved.reshape(residual_ref.shape)
    hidden_ref[...] = summed.astype(BF16)
    mean_square = jnp.mean(summed * summed, axis=-1, keepdims=True)
    scale = lax.rsqrt(mean_square + 1e-05)
    normed_ref[...] = (summed * scale * gain_ref[...].astype(F32)[None, None]).astype(BF16)


def body(
    queries,
    new_keys,
    incoming_values,
    request_cached_keys,
    request_cached_values,
    cache_lengths,
    out_weight,
    residual,
    norm_gain,
):
    gathered = spread(
        queries,
        new_keys,
        incoming_values,
        request_cached_keys,
        request_cached_values,
        cache_lengths,
        out_weight,
    )
    positions, requests, width = residual.shape
    lines = 32
    block = pl.BlockSpec((positions, lines, width), lambda i: (0, i, 0))
    out = jax.ShapeDtypeStruct(residual.shape, BF16)
    hidden, normed = pl.pallas_call(
        norm_kernel,
        grid=(requests // lines,),
        in_specs=[
            pl.BlockSpec((positions * lines, width), lambda i: (i, 0)),
            block,
            pl.BlockSpec((width,), lambda i: (0,)),
        ],
        out_specs=[block, block],
        out_shape=[out, out],
        compiler_params=pltpu.CompilerParams(vmem_limit_bytes=63 << 20),
    )(gathered, residual, norm_gain)
    return hidden, normed


def solution(mesh):
    placed = (
        P("req", None, "head"),
        P("req", None, "head"),
        P("req", None, "head"),
        P("req", None, "head"),
        P("req", None, "head"),
        P("req"),
        P("head", None),
        P(("req", "head"), None, None),
        P(),
    )
    return jax.shard_map(
        body,
        mesh=mesh,
        in_specs=placed,
        out_specs=(P(("req", "head"), None, None), P(("req", "head"), None, None)),
        check_vma=False,
    )
```

```python
import functools
import math

import jax
import jax.numpy as jnp
from jax import lax
from jax.experimental import pallas as pl
from jax.experimental.pallas import tpu as pltpu
from jax.sharding import PartitionSpec as P

HEAD_SIZE = 128
NEGATIVE_FILLER = -1e30
K_BLOCK = 512
N_TILE = 512
LOG2_SCALE = math.log2(math.e) / math.sqrt(HEAD_SIZE)
BF16, F32 = jnp.bfloat16, jnp.float32
MESH = pl.DeviceIdType.MESH


def spread_kernel(
    sizes,
    length_ref,
    q_hbm,
    new_k_hbm,
    new_v_hbm,
    key_hbm,
    value_hbm,
    weight_hbm,
    gathered,
    query,
    new_keys,
    keys,
    values,
    weight,
    pair_weight,
    attended,
    rows_of_owner,
    part,
    far_in,
    near_in,
    pair_rows,
    mixed,
    wide_part,
    wide_in,
    summed,
    load_sem,
    weight_sem,
    piece_send,
    piece_recv,
    rows_send,
    rows_recv,
    wide_send,
    wide_recv,
    far_send,
    far_recv,
    near_send,
    near_recv,
    out_send,
    out_recv,
    self_sem,
):
    req_count, head_count, requests, key_heads, members = sizes
    row = lax.axis_index("req")
    me = lax.axis_index("head")
    pair = me + 1 - 2 * lax.rem(me, 2)
    across = head_count - 1 - me
    opposite = head_count - 1 - pair
    sides = (pair, across)
    chunks = part.shape[0]
    slots, span = key_hbm.shape[1], new_k_hbm.shape[1]
    narrow = part.shape[3]
    half = narrow // 2
    lane_groups = [pl.ds(g * HEAD_SIZE, HEAD_SIZE) for g in range(key_heads)]

    barrier = pltpu.get_barrier_semaphore()
    for neighbour in sides:
        pl.semaphore_signal(barrier, inc=1, device_id=(row, neighbour), device_id_type=MESH)

    def greet(step, carried):
        peer = lax.rem(row + step, req_count)
        pl.semaphore_signal(barrier, inc=1, device_id=(peer, me), device_id_type=MESH)
        return carried

    lax.fori_loop(1, req_count, greet, 0)

    for r in range(requests):
        for g in range(key_heads):
            values[r, g, :, HEAD_SIZE:] = jnp.ones((slots + span, HEAD_SIZE), BF16)

    def loads(r):
        pairs = [
            (q_hbm.at[r], query.at[r]),
            (key_hbm.at[r], keys.at[r]),
            (new_k_hbm.at[r], new_keys.at[r]),
        ]
        for g, lanes in enumerate(lane_groups):
            old = values.at[r, g, pl.ds(0, slots), pl.ds(0, HEAD_SIZE)]
            new = values.at[r, g, pl.ds(slots, span), pl.ds(0, HEAD_SIZE)]
            pairs += [(value_hbm.at[r, :, lanes], old), (new_v_hbm.at[r, :, lanes], new)]
        return [
            pltpu.make_async_copy(source, target, load_sem.at[r, i])
            for i, (source, target) in enumerate(pairs)
        ]

    for r in range(requests):
        for copy in loads(r):
            copy.start()
    weight_load = pltpu.make_async_copy(weight_hbm, weight, weight_sem)
    weight_load.start()

    depth = weight.shape[0] // 2
    share = depth // req_count
    core = lax.rem(row, 2)
    sibling = row + 1 - 2 * core

    def place_of(along_y, along_z):
        y = lax.rem(row // 8 + along_y, 4)
        z = lax.rem(lax.rem(row // 2, 4) + along_z, 4)
        return y * 8 + z * 2 + core

    def along(order, first, second):
        return place_of(first, second) if order == 0 else place_of(second, first)

    def give(order, piece, slot, device, source=None):
        lines = pl.ds(pl.multiple_of(order * depth + piece * share, share), share)
        return pltpu.make_async_remote_copy(
            src_ref=pair_weight.at[lines] if source is None else weight_hbm.at[lines, pl.ds(narrow, narrow)],
            dst_ref=pair_weight.at[lines],
            send_sem=piece_send.at[order, slot],
            recv_sem=piece_recv.at[order, piece],
            device_id=device,
            device_id_type=MESH,
        )

    def take(order, piece):
        give(order, piece, 0, (sibling, me)).wait_recv()

    def fetch_pieces():
        for order in range(2):
            give(order, row, 0, (row, pair), weight_hbm).start()

    def first_line():
        for order in range(2):
            take(order, row)
            for k in range(1, 4):
                give(order, row, k, (along(order, k, 0), me)).start()

    def second_line():
        for order in range(2):
            for j in range(4):
                piece = along(order, j, 0)
                if j:
                    take(order, piece)
                for k in range(1, 4):
                    give(order, piece, 3 + j * 3 + k, (along(order, 0, k), me)).start()

    def to_sibling():
        for order in range(2):

            def one(n, carried, order=order):
                piece = along(order, lax.rem(n, 4), n // 4)
                pl.when(n >= 4)(lambda: take(order, piece))
                give(order, piece, 16 + n, (sibling, me)).start()
                return carried

            lax.fori_loop(0, 16, one, 0)

    def from_sibling():
        for order in range(2):

            def one(n, carried, order=order):
                take(order, along(order, lax.rem(n, 4), n // 4) + 1 - 2 * core)
                return carried

            lax.fori_loop(0, 16, one, 0)

    def pieces_sent():
        for order in range(2):
            give(order, row, 0, (row, pair), weight_hbm).wait_send()

            def one(n, carried, order=order):
                give(order, row, n, (sibling, me)).wait_send()
                return carried

            lax.fori_loop(1, 32, one, 0)

    contract_last = (((1,), (1,)), ((), ()))

    def attend(turn, r):
        length = length_ref[r]
        tile = query.shape[1] * 16
        stacked = members * tile
        for g in range(key_heads):
            lanes = pl.ds(g * members * HEAD_SIZE, members * HEAD_SIZE)
            rows = query[r, :, pl.ds(pl.multiple_of(turn * 16, 16), 16), lanes]
            rows = rows.reshape(tile, members * HEAD_SIZE)
            q = jnp.concatenate(
                [rows[:, j * HEAD_SIZE : (j + 1) * HEAD_SIZE] for j in range(members)], axis=0
            )
            running_max = total = None
            for at in range(0, slots + span, K_BLOCK):
                cached = at < slots
                if cached:
                    k = keys[r, at : at + K_BLOCK, g * HEAD_SIZE : (g + 1) * HEAD_SIZE]
                else:
                    k = new_keys[r, at - slots : at - slots + K_BLOCK, g * HEAD_SIZE : (g + 1) * HEAD_SIZE]
                scores = lax.dot_general(q, k, contract_last, preferred_element_type=F32)
                if cached:
                    slot = lax.broadcasted_iota(jnp.int32, (1, K_BLOCK), 1) + at
                    scores = scores + jnp.where(slot < length, 0.0, NEGATIVE_FILLER)
                else:
                    line = lax.broadcasted_iota(jnp.int32, (stacked, K_BLOCK), 0)
                    block = (line >> 4) & (query.shape[1] - 1)
                    position = block * query.shape[2] + (line & 15) + turn * 16
                    column = lax.broadcasted_iota(jnp.int32, (stacked, K_BLOCK), 1) + (at - slots)
                    scores = jnp.where(column <= position, scores, NEGATIVE_FILLER)
                block_max = jnp.max(scores, axis=1, keepdims=True)
                new_max = block_max if total is None else jnp.maximum(running_max, block_max)
                weights = jnp.exp2((scores - new_max) * LOG2_SCALE).astype(BF16)
                product = jnp.dot(weights, values[r, g, at : at + K_BLOCK], preferred_element_type=F32)
                if total is None:
                    total = product
                else:
                    total = total * jnp.exp2((running_max - new_max) * LOG2_SCALE) + product
                running_max = new_max
            out = total[:, :HEAD_SIZE] / total[:, HEAD_SIZE:]
            for j in range(members):
                at = (g * members + j) * HEAD_SIZE
                attended[r, :, at : at + HEAD_SIZE] = out[j * tile : (j + 1) * tile]

    def order_rows(c):
        count = attended.shape[1] // 8
        shape = (count, 8, attended.shape[2])
        first, second = attended[0].reshape(shape), attended[1].reshape(shape)
        upper = lax.broadcasted_iota(jnp.int32, shape, 1) < 4
        even = jnp.where(upper, first, pltpu.roll(second, 4, 1))
        odd = jnp.where(upper, pltpu.roll(first, 4, 1), second)
        for low, rows in enumerate((even, odd)):
            split = rows.reshape(count // 2, 2, 8, shape[2])
            for high in range(2):
                owner = 2 * high + low
                lines = split[:, high].reshape(count * 4, shape[2]).astype(BF16)
                rows_of_owner[c, owner] = lines

    def project(c, first):
        def tile(n, carried):
            columns = pl.ds(pl.multiple_of(n * N_TILE, N_TILE), N_TILE)
            rows = rows_of_owner[c].reshape(-1, weight.shape[0])
            product = jnp.dot(rows, weight[:, columns], preferred_element_type=F32)
            part[c, :, :, columns] = product.astype(BF16).reshape(head_count, -1, N_TILE)
            return carried

        tiles = half // N_TILE
        lax.fori_loop(first * tiles, (first + 1) * tiles, tile, 0)

    def lend(c, which):
        return pltpu.make_async_remote_copy(
            src_ref=rows_of_owner.at[c, (pair, opposite)[which]],
            dst_ref=pair_rows.at[c, which],
            send_sem=rows_send.at[c, which],
            recv_sem=rows_recv.at[c, which],
            device_id=(row, pair),
            device_id_type=MESH,
        )

    def hand_across(c):
        return pltpu.make_async_remote_copy(
            src_ref=wide_part.at[c, 1],
            dst_ref=wide_in.at[c],
            send_sem=wide_send.at[c],
            recv_sem=wide_recv.at[c],
            device_id=(row, across),
            device_id_type=MESH,
        )

    def project_both(pairing, carried):
        inner = weight.shape[0]
        lines = rows_of_owner.shape[2]
        for i in range(2):
            c = 2 * pairing + i
            for which, owner in enumerate((me, across)):
                lend(c, which).wait_recv()
                at = (2 * i + which) * lines
                mixed[at : at + lines, :inner] = rows_of_owner[c, owner]
                mixed[at : at + lines, inner:] = pair_rows[c, which]

        def tile(n, inner_carried):
            columns = pl.ds(pl.multiple_of(n * N_TILE, N_TILE), N_TILE)
            own_columns = pl.ds(pl.multiple_of(narrow + n * N_TILE, N_TILE), N_TILE)
            product = jnp.dot(mixed[:, :inner], weight[:, own_columns], preferred_element_type=F32)
            product += jnp.dot(mixed[:, inner:], pair_weight[:, columns], preferred_element_type=F32)
            block = product.astype(BF16).reshape(2, 2, lines, N_TILE)
            wide_part[pl.ds(2 * pairing, 2), :, :, columns] = block
            return inner_carried

        lax.fori_loop(0, narrow // N_TILE, tile, 0)
        for i in range(2):
            hand_across(2 * pairing + i).start()
        return carried

    def far(c, side):
        return pltpu.make_async_remote_copy(
            src_ref=part.at[c, opposite, :, pl.ds(side * half, half)],
            dst_ref=far_in.at[c, side],
            send_sem=far_send.at[c, side],
            recv_sem=far_recv.at[c, side],
            device_id=(row, sides[side]),
            device_id_type=MESH,
        )

    def near(c, side, summed_half):
        columns = pl.ds((1 - side if summed_half else side) * half, half)
        return pltpu.make_async_remote_copy(
            src_ref=part.at[c, sides[side], :, columns],
            dst_ref=near_in.at[c, side, :, columns],
            send_sem=near_send.at[c, side, int(summed_half)],
            recv_sem=near_recv.at[c, side, int(summed_half)],
            device_id=(row, sides[side]),
            device_id_type=MESH,
        )

    def pass_on(c):
        for side in range(2):
            far(c, side).wait_recv()
            target = sides[1 - side]
            columns = pl.ds(side * half, half)
            own = part[c, target, :, columns].astype(F32)
            part[c, target, :, columns] = (own + far_in[c, side].astype(F32)).astype(BF16)
            if side == 0:
                near(c, 1, True).start()

    def to_pair(c):
        near(c, 0, False).start()
        near(c, 0, True).start()

    group, place = row // chunks, lax.rem(row, chunks)
    groups = req_count // chunks

    def finish(c, kept=False):
        for side in range(2):
            near(c, side, False).wait_recv()
            near(c, side, True).wait_recv()
        total = part[c, me].astype(F32) + near_in[c, 0].astype(F32) + near_in[c, 1].astype(F32)
        shape = summed.shape[1:3] + (narrow,)
        summed[c, :, :, :narrow] = total.reshape(shape).astype(BF16)
        hand_across(c).wait_recv()
        total = wide_part[c, 0].astype(F32) + wide_in[c].astype(F32)
        summed[c, :, :, narrow:] = total.reshape(shape).astype(BF16)

        def send(step, carried):
            outgoing(c, step).start()
            return carried

        if kept:
            keep().start()
        lax.fori_loop(1 if kept else 0, groups, send, 0)

    def outgoing(c, step):
        block = lax.rem(group + step, groups)
        target = block * chunks + lax.rem(place + c, chunks)
        return pltpu.make_async_remote_copy(
            src_ref=summed.at[c, block],
            dst_ref=gathered.at[pl.ds(pl.multiple_of(row * 8, 8), 8)],
            send_sem=out_send.at[c, step],
            recv_sem=out_recv.at[row],
            device_id=(target, me),
            device_id_type=MESH,
        )

    def keep():
        lines = gathered.at[pl.ds(pl.multiple_of(row * 8, 8), 8)]
        return pltpu.make_async_copy(summed.at[0, group], lines, self_sem)

    def half_chunk(step, carried):
        c, r = lax.div(step, requests), lax.rem(step, requests)

        @pl.when(step == 0)
        def _():
            pl.semaphore_wait(barrier, 2 + req_count - 1)
            fetch_pieces()

        pl.when(step == 2)(first_line)
        pl.when(step == 5)(second_line)
        pl.when(step == 12)(to_sibling)

        @pl.when(c == 0)
        def _():
            for copy in loads(r):
                copy.wait()

        attend(lax.rem(place + c, chunks), r)

        @pl.when(r == requests - 1)
        def _():
            pl.when(c > 0)(lambda: pass_on(c - 1))
            order_rows(c)
            for which in range(2):
                lend(c, which).start()

            @pl.when(c == 0)
            def _():
                weight_load.wait()

            for side in range(2):
                project(c, side)
                far(c, side).start()
            near(c, 1, False).start()

        return carried

    lax.fori_loop(0, chunks * requests, half_chunk, 0)

    def early(c, carried):
        to_pair(c)
        return carried

    lax.fori_loop(0, chunks - 1, early, 0)
    from_sibling()
    lax.fori_loop(0, chunks // 4, project_both, 0)
    pass_on(chunks - 1)
    to_pair(chunks - 1)
    lax.fori_loop(chunks // 4, chunks // 2, project_both, 0)
    finish(0, True)

    def rest(c, carried):
        finish(c)
        return carried

    lax.fori_loop(1, chunks, rest, 0)

    keep().wait()
    pieces_sent()
    for c in range(chunks):
        for side in range(2):
            lend(c, side).wait_send()
            far(c, side).wait_send()
            near(c, side, False).wait_send()
            near(c, side, True).wait_send()
        hand_across(c).wait_send()

        def sent(step, carried, c=c):
            outgoing(c, step).wait_send()
            return carried

        lax.fori_loop(1 if c == 0 else 0, groups, sent, 0)

    def arrived(step, carried):
        source = lax.rem(row + step, req_count)
        lines = gathered.at[pl.ds(pl.multiple_of(source * 8, 8), 8)]
        pltpu.make_async_remote_copy(
            src_ref=summed.at[0, 0],
            dst_ref=lines,
            send_sem=out_send.at[0, 0],
            recv_sem=out_recv.at[source],
            device_id=(source, me),
            device_id_type=MESH,
        ).wait_recv()
        return carried

    lax.fori_loop(1, req_count, arrived, 0)


def spread(queries, new_keys, new_values, cached_keys, cached_values, lengths, weight):
    requests, span, q_width = queries.shape
    slots, kv_width = cached_keys.shape[1:]
    key_heads = kv_width // HEAD_SIZE
    members = q_width // kv_width
    width = weight.shape[1]
    req_count, head_count = lax.axis_size("req"), lax.axis_size("head")
    chunks = 8
    blocks = req_count // chunks
    tile = blocks * 16
    lines = blocks * 8
    narrow = width // 2
    anywhere = pl.BlockSpec(memory_space=pl.ANY)
    dma = pltpu.SemaphoreType.DMA
    return pl.pallas_call(
        functools.partial(spread_kernel, (req_count, head_count, requests, key_heads, members)),
        in_specs=[pl.BlockSpec(memory_space=pltpu.SMEM)] + [anywhere] * 6,
        out_specs=anywhere,
        out_shape=jax.ShapeDtypeStruct((req_count * 8, width), BF16),
        scratch_shapes=[
            pltpu.VMEM((requests, blocks, span // blocks, q_width), BF16),
            pltpu.VMEM((requests, span, kv_width), BF16),
            pltpu.VMEM((requests, slots, kv_width), BF16),
            pltpu.VMEM((requests, key_heads, slots + span, 2 * HEAD_SIZE), BF16),
            pltpu.VMEM(weight.shape, BF16),
            pltpu.VMEM((q_width, narrow), BF16),
            pltpu.VMEM((requests, tile, q_width), F32),
            pltpu.VMEM((chunks, head_count, lines, q_width), BF16),
            pltpu.VMEM((chunks, head_count, lines, narrow), BF16),
            pltpu.VMEM((chunks, 2, lines, narrow // 2), BF16),
            pltpu.VMEM((chunks, 2, lines, narrow), BF16),
            pltpu.VMEM((chunks, 2, lines, q_width), BF16),
            pltpu.VMEM((4 * lines, 2 * q_width), BF16),
            pltpu.VMEM((chunks, 2, lines, narrow), BF16),
            pltpu.VMEM((chunks, lines, narrow), BF16),
            pltpu.VMEM((chunks, blocks, 8, width), BF16),
            dma((requests, 3 + 2 * key_heads)),
            dma,
            dma((2, 32)),
            dma((2, req_count)),
            dma((chunks, 2)),
            dma((chunks, 2)),
            dma((chunks,)),
            dma((chunks,)),
            dma((chunks, 2)),
            dma((chunks, 2)),
            dma((chunks, 2, 2)),
            dma((chunks, 2, 2)),
            dma((chunks, blocks)),
            dma((req_count,)),
            dma,
        ],
        compiler_params=pltpu.CompilerParams(
            collective_id=0, has_side_effects=True, vmem_limit_bytes=63 << 20
        ),
    )(
        lengths,
        queries.reshape(requests, blocks, span // blocks, q_width),
        new_keys,
        new_values,
        cached_keys,
        cached_values,
        weight,
    )


def norm_kernel(rows_ref, residual_ref, gain_ref, hidden_ref, normed_ref):
    count = rows_ref.shape[0]
    positions = residual_ref.shape[0]
    lines = residual_ref.shape[1]
    target = lax.broadcasted_iota(jnp.int32, (count, count), 0)
    source = lax.broadcasted_iota(jnp.int32, (count, count), 1)
    wanted = (target & (lines - 1)) * positions + (target >> (lines.bit_length() - 1))
    pick = (source == wanted).astype(F32).astype(BF16)
    moved = jnp.dot(pick, rows_ref[...], preferred_element_type=F32)
    summed = residual_ref[...].astype(F32) + moved.reshape(residual_ref.shape)
    hidden_ref[...] = summed.astype(BF16)
    mean_square = jnp.mean(summed * summed, axis=-1, keepdims=True)
    scale = lax.rsqrt(mean_square + 1e-05)
    normed_ref[...] = (summed * scale * gain_ref[...].astype(F32)[None, None]).astype(BF16)


def body(
    queries,
    new_keys,
    incoming_values,
    request_cached_keys,
    request_cached_values,
    cache_lengths,
    out_weight,
    residual,
    norm_gain,
):
    gathered = spread(
        queries,
        new_keys,
        incoming_values,
        request_cached_keys,
        request_cached_values,
        cache_lengths,
        out_weight,
    )
    positions, requests, width = residual.shape
    lines = 32
    block = pl.BlockSpec((positions, lines, width), lambda i: (0, i, 0))
    out = jax.ShapeDtypeStruct(residual.shape, BF16)
    hidden, normed = pl.pallas_call(
        norm_kernel,
        grid=(requests // lines,),
        in_specs=[
            pl.BlockSpec((positions * lines, width), lambda i: (i, 0)),
            block,
            pl.BlockSpec((width,), lambda i: (0,)),
        ],
        out_specs=[block, block],
        out_shape=[out, out],
        compiler_params=pltpu.CompilerParams(vmem_limit_bytes=63 << 20),
    )(gathered, residual, norm_gain)
    return hidden, normed


def solution(mesh):
    placed = (
        P("req", None, "head"),
        P("req", None, "head"),
        P("req", None, "head"),
        P("req", None, "head"),
        P("req", None, "head"),
        P("req"),
        P("head", None),
        P(("req", "head"), None, None),
        P(),
    )
    return jax.shard_map(
        body,
        mesh=mesh,
        in_specs=placed,
        out_specs=(P(("req", "head"), None, None), P(("req", "head"), None, None)),
        check_vma=False,
    )
```

```python
import functools
import math

import jax
import jax.numpy as jnp
from jax import lax
from jax.experimental import pallas as pl
from jax.experimental.pallas import tpu as pltpu
from jax.sharding import PartitionSpec as P

HEAD_SIZE = 128
NEGATIVE_FILLER = -1e30
K_BLOCK = 512
N_TILE = 512
LOG2_SCALE = math.log2(math.e) / math.sqrt(HEAD_SIZE)
BF16, F32 = jnp.bfloat16, jnp.float32
MESH = pl.DeviceIdType.MESH


def spread_kernel(
    sizes,
    length_ref,
    q_hbm,
    new_k_hbm,
    new_v_hbm,
    key_hbm,
    value_hbm,
    weight_hbm,
    gathered,
    query,
    new_keys,
    keys,
    values,
    weight,
    pair_weight,
    attended,
    rows_of_owner,
    part,
    far_in,
    near_in,
    pair_rows,
    mixed,
    wide_part,
    wide_in,
    summed,
    load_sem,
    weight_sem,
    piece_send,
    piece_recv,
    rows_send,
    rows_recv,
    wide_send,
    wide_recv,
    far_send,
    far_recv,
    near_send,
    near_recv,
    out_send,
    out_recv,
    self_sem,
):
    req_count, head_count, requests, key_heads, members = sizes
    row = lax.axis_index("req")
    me = lax.axis_index("head")
    pair = me + 1 - 2 * lax.rem(me, 2)
    across = head_count - 1 - me
    opposite = head_count - 1 - pair
    sides = (pair, across)
    chunks = part.shape[0]
    slots, span = key_hbm.shape[1], new_k_hbm.shape[1]
    narrow = part.shape[3]
    half = narrow // 2
    lane_groups = [pl.ds(g * HEAD_SIZE, HEAD_SIZE) for g in range(key_heads)]

    barrier = pltpu.get_barrier_semaphore()
    for neighbour in sides:
        pl.semaphore_signal(barrier, inc=1, device_id=(row, neighbour), device_id_type=MESH)

    def greet(step, carried):
        peer = lax.rem(row + step, req_count)
        pl.semaphore_signal(barrier, inc=1, device_id=(peer, me), device_id_type=MESH)
        return carried

    lax.fori_loop(1, req_count, greet, 0)

    for r in range(requests):
        for g in range(key_heads):
            values[r, g, :, HEAD_SIZE:] = jnp.ones((slots + span, HEAD_SIZE), BF16)

    def loads(r):
        pairs = [
            (q_hbm.at[r], query.at[r]),
            (key_hbm.at[r], keys.at[r]),
            (new_k_hbm.at[r], new_keys.at[r]),
        ]
        for g, lanes in enumerate(lane_groups):
            old = values.at[r, g, pl.ds(0, slots), pl.ds(0, HEAD_SIZE)]
            new = values.at[r, g, pl.ds(slots, span), pl.ds(0, HEAD_SIZE)]
            pairs += [(value_hbm.at[r, :, lanes], old), (new_v_hbm.at[r, :, lanes], new)]
        return [
            pltpu.make_async_copy(source, target, load_sem.at[r, i])
            for i, (source, target) in enumerate(pairs)
        ]

    for r in range(requests):
        for copy in loads(r):
            copy.start()
    weight_load = pltpu.make_async_copy(weight_hbm, weight, weight_sem)
    weight_load.start()

    depth = weight.shape[0] // 2
    share = depth // req_count
    core = lax.rem(row, 2)
    sibling = row + 1 - 2 * core

    def place_of(along_y, along_z):
        y = lax.rem(row // 8 + along_y, 4)
        z = lax.rem(lax.rem(row // 2, 4) + along_z, 4)
        return y * 8 + z * 2 + core

    def along(order, first, second):
        return place_of(first, second) if order == 0 else place_of(second, first)

    def give(order, piece, slot, device, source=None):
        lines = pl.ds(pl.multiple_of(order * depth + piece * share, share), share)
        return pltpu.make_async_remote_copy(
            src_ref=pair_weight.at[lines] if source is None else weight_hbm.at[lines, pl.ds(narrow, narrow)],
            dst_ref=pair_weight.at[lines],
            send_sem=piece_send.at[order, slot],
            recv_sem=piece_recv.at[order, piece],
            device_id=device,
            device_id_type=MESH,
        )

    def take(order, piece):
        give(order, piece, 0, (sibling, me)).wait_recv()

    def fetch_pieces():
        for order in range(2):
            give(order, row, 0, (row, pair), weight_hbm).start()

    def first_line():
        for order in range(2):
            take(order, row)
            for k in range(1, 4):
                give(order, row, k, (along(order, k, 0), me)).start()

    def second_line():
        for order in range(2):
            for j in range(4):
                piece = along(order, j, 0)
                if j:
                    take(order, piece)
                for k in range(1, 4):
                    give(order, piece, 3 + j * 3 + k, (along(order, 0, k), me)).start()

    def to_sibling():
        for order in range(2):

            def one(n, carried, order=order):
                piece = along(order, lax.rem(n, 4), n // 4)
                pl.when(n >= 4)(lambda: take(order, piece))
                give(order, piece, 16 + n, (sibling, me)).start()
                return carried

            lax.fori_loop(0, 16, one, 0)

    def from_sibling():
        for order in range(2):

            def one(n, carried, order=order):
                take(order, along(order, lax.rem(n, 4), n // 4) + 1 - 2 * core)
                return carried

            lax.fori_loop(0, 16, one, 0)

    def pieces_sent():
        for order in range(2):
            give(order, row, 0, (row, pair), weight_hbm).wait_send()

            def one(n, carried, order=order):
                give(order, row, n, (sibling, me)).wait_send()
                return carried

            lax.fori_loop(1, 32, one, 0)

    contract_last = (((1,), (1,)), ((), ()))

    def attend(turn, r):
        length = length_ref[r]
        tile = query.shape[1] * 16
        stacked = members * tile
        for g in range(key_heads):
            lanes = pl.ds(g * members * HEAD_SIZE, members * HEAD_SIZE)
            rows = query[r, :, pl.ds(pl.multiple_of(turn * 16, 16), 16), lanes]
            rows = rows.reshape(tile, members * HEAD_SIZE)
            q = jnp.concatenate(
                [rows[:, j * HEAD_SIZE : (j + 1) * HEAD_SIZE] for j in range(members)], axis=0
            )
            running_max = total = None
            for at in range(0, slots + span, K_BLOCK):
                cached = at < slots
                if cached:
                    k = keys[r, at : at + K_BLOCK, g * HEAD_SIZE : (g + 1) * HEAD_SIZE]
                else:
                    k = new_keys[r, at - slots : at - slots + K_BLOCK, g * HEAD_SIZE : (g + 1) * HEAD_SIZE]
                scores = lax.dot_general(q, k, contract_last, preferred_element_type=F32)
                if cached:
                    slot = lax.broadcasted_iota(jnp.int32, (1, K_BLOCK), 1) + at
                    scores = scores + jnp.where(slot < length, 0.0, NEGATIVE_FILLER)
                else:
                    line = lax.broadcasted_iota(jnp.int32, (stacked, K_BLOCK), 0)
                    block = (line >> 4) & (query.shape[1] - 1)
                    position = block * query.shape[2] + (line & 15) + turn * 16
                    column = lax.broadcasted_iota(jnp.int32, (stacked, K_BLOCK), 1) + (at - slots)
                    scores = jnp.where(column <= position, scores, NEGATIVE_FILLER)
                block_max = jnp.max(scores, axis=1, keepdims=True)
                new_max = block_max if total is None else jnp.maximum(running_max, block_max)
                weights = jnp.exp2((scores - new_max) * LOG2_SCALE).astype(BF16)
                product = jnp.dot(weights, values[r, g, at : at + K_BLOCK], preferred_element_type=F32)
                if total is None:
                    total = product
                else:
                    total = total * jnp.exp2((running_max - new_max) * LOG2_SCALE) + product
                running_max = new_max
            out = total[:, :HEAD_SIZE] / total[:, HEAD_SIZE:]
            for j in range(members):
                at = (g * members + j) * HEAD_SIZE
                attended[r, :, at : at + HEAD_SIZE] = out[j * tile : (j + 1) * tile]

    def order_rows(c):
        count = attended.shape[1] // 8
        shape = (count, 8, attended.shape[2])
        first, second = attended[0].reshape(shape), attended[1].reshape(shape)
        upper = lax.broadcasted_iota(jnp.int32, shape, 1) < 4
        even = jnp.where(upper, first, pltpu.roll(second, 4, 1))
        odd = jnp.where(upper, pltpu.roll(first, 4, 1), second)
        for low, rows in enumerate((even, odd)):
            split = rows.reshape(count // 2, 2, 8, shape[2])
            for high in range(2):
                owner = 2 * high + low
                lines = split[:, high].reshape(count * 4, shape[2]).astype(BF16)
                rows_of_owner[c, owner] = lines

    def project(c, first):
        def tile(n, carried):
            columns = pl.ds(pl.multiple_of(n * N_TILE, N_TILE), N_TILE)
            rows = rows_of_owner[c].reshape(-1, weight.shape[0])
            product = jnp.dot(rows, weight[:, columns], preferred_element_type=F32)
            part[c, :, :, columns] = product.astype(BF16).reshape(head_count, -1, N_TILE)
            return carried

        tiles = half // N_TILE
        lax.fori_loop(first * tiles, (first + 1) * tiles, tile, 0)

    def lend(c, which):
        return pltpu.make_async_remote_copy(
            src_ref=rows_of_owner.at[c, (pair, opposite)[which]],
            dst_ref=pair_rows.at[c, which],
            send_sem=rows_send.at[c, which],
            recv_sem=rows_recv.at[c, which],
            device_id=(row, pair),
            device_id_type=MESH,
        )

    def hand_across(c):
        return pltpu.make_async_remote_copy(
            src_ref=wide_part.at[c, 1],
            dst_ref=wide_in.at[c],
            send_sem=wide_send.at[c],
            recv_sem=wide_recv.at[c],
            device_id=(row, across),
            device_id_type=MESH,
        )

    def project_both(pairing, carried):
        inner = weight.shape[0]
        lines = rows_of_owner.shape[2]
        for i in range(2):
            c = 2 * pairing + i
            for which, owner in enumerate((me, across)):
                lend(c, which).wait_recv()
                at = (2 * i + which) * lines
                mixed[at : at + lines, :inner] = rows_of_owner[c, owner]
                mixed[at : at + lines, inner:] = pair_rows[c, which]

        def tile(n, inner_carried):
            columns = pl.ds(pl.multiple_of(n * N_TILE, N_TILE), N_TILE)
            own_columns = pl.ds(pl.multiple_of(narrow + n * N_TILE, N_TILE), N_TILE)
            product = jnp.dot(mixed[:, :inner], weight[:, own_columns], preferred_element_type=F32)
            product += jnp.dot(mixed[:, inner:], pair_weight[:, columns], preferred_element_type=F32)
            block = product.astype(BF16).reshape(2, 2, lines, N_TILE)
            wide_part[pl.ds(2 * pairing, 2), :, :, columns] = block
            return inner_carried

        lax.fori_loop(0, narrow // N_TILE, tile, 0)
        for i in range(2):
            hand_across(2 * pairing + i).start()
        return carried

    def far(c, side):
        return pltpu.make_async_remote_copy(
            src_ref=part.at[c, opposite, :, pl.ds(side * half, half)],
            dst_ref=far_in.at[c, side],
            send_sem=far_send.at[c, side],
            recv_sem=far_recv.at[c, side],
            device_id=(row, sides[side]),
            device_id_type=MESH,
        )

    def near(c, side, summed_half):
        columns = pl.ds((1 - side if summed_half else side) * half, half)
        return pltpu.make_async_remote_copy(
            src_ref=part.at[c, sides[side], :, columns],
            dst_ref=near_in.at[c, side, :, columns],
            send_sem=near_send.at[c, side, int(summed_half)],
            recv_sem=near_recv.at[c, side, int(summed_half)],
            device_id=(row, sides[side]),
            device_id_type=MESH,
        )

    def pass_on(c):
        for side in range(2):
            far(c, side).wait_recv()
            target = sides[1 - side]
            columns = pl.ds(side * half, half)
            own = part[c, target, :, columns].astype(F32)
            part[c, target, :, columns] = (own + far_in[c, side].astype(F32)).astype(BF16)
            if side == 0:
                near(c, 1, True).start()

    def to_pair(c):
        near(c, 0, False).start()
        near(c, 0, True).start()

    group, place = row // chunks, lax.rem(row, chunks)
    groups = req_count // chunks

    def finish(c, kept=False):
        for side in range(2):
            near(c, side, False).wait_recv()
            near(c, side, True).wait_recv()
        total = part[c, me].astype(F32) + near_in[c, 0].astype(F32) + near_in[c, 1].astype(F32)
        shape = summed.shape[1:3] + (narrow,)
        summed[c, :, :, :narrow] = total.reshape(shape).astype(BF16)
        hand_across(c).wait_recv()
        total = wide_part[c, 0].astype(F32) + wide_in[c].astype(F32)
        summed[c, :, :, narrow:] = total.reshape(shape).astype(BF16)

        def send(step, carried):
            outgoing(c, step).start()
            return carried

        if kept:
            keep().start()
        lax.fori_loop(1 if kept else 0, groups, send, 0)

    def outgoing(c, step):
        block = lax.rem(group + step, groups)
        target = block * chunks + lax.rem(place + c, chunks)
        return pltpu.make_async_remote_copy(
            src_ref=summed.at[c, block],
            dst_ref=gathered.at[pl.ds(pl.multiple_of(row * 8, 8), 8)],
            send_sem=out_send.at[c, step],
            recv_sem=out_recv.at[row],
            device_id=(target, me),
            device_id_type=MESH,
        )

    def keep():
        lines = gathered.at[pl.ds(pl.multiple_of(row * 8, 8), 8)]
        return pltpu.make_async_copy(summed.at[0, group], lines, self_sem)

    def half_chunk(step, carried):
        c, r = lax.div(step, requests), lax.rem(step, requests)

        @pl.when(step == 0)
        def _():
            pl.semaphore_wait(barrier, 2 + req_count - 1)
            fetch_pieces()

        pl.when(step == 2)(first_line)
        pl.when(step == 5)(second_line)
        pl.when(step == 12)(to_sibling)

        @pl.when(c == 0)
        def _():
            for copy in loads(r):
                copy.wait()

        attend(lax.rem(place + c, chunks), r)

        @pl.when(r == requests - 1)
        def _():
            pl.when(c > 0)(lambda: pass_on(c - 1))
            order_rows(c)
            for which in range(2):
                lend(c, which).start()

            @pl.when(c == 0)
            def _():
                weight_load.wait()

            for side in range(2):
                project(c, side)
                far(c, side).start()
            near(c, 1, False).start()

        return carried

    lax.fori_loop(0, chunks * requests, half_chunk, 0)

    def early(c, carried):
        to_pair(c)
        return carried

    lax.fori_loop(0, chunks - 1, early, 0)
    from_sibling()
    project_both(0, 0)
    pass_on(chunks - 1)
    to_pair(chunks - 1)
    project_both(1, 0)
    finish(0, True)
    finish(1)

    def both_and_finish(pairing, carried):
        project_both(pairing, carried)
        finish(2 * pairing - 2)
        finish(2 * pairing - 1)
        return carried

    lax.fori_loop(2, chunks // 2, both_and_finish, 0)
    finish(chunks - 2)
    finish(chunks - 1)

    keep().wait()
    pieces_sent()
    for c in range(chunks):
        for side in range(2):
            lend(c, side).wait_send()
            far(c, side).wait_send()
            near(c, side, False).wait_send()
            near(c, side, True).wait_send()
        hand_across(c).wait_send()

        def sent(step, carried, c=c):
            outgoing(c, step).wait_send()
            return carried

        lax.fori_loop(1 if c == 0 else 0, groups, sent, 0)

    def arrived(step, carried):
        source = lax.rem(row + step, req_count)
        lines = gathered.at[pl.ds(pl.multiple_of(source * 8, 8), 8)]
        pltpu.make_async_remote_copy(
            src_ref=summed.at[0, 0],
            dst_ref=lines,
            send_sem=out_send.at[0, 0],
            recv_sem=out_recv.at[source],
            device_id=(source, me),
            device_id_type=MESH,
        ).wait_recv()
        return carried

    lax.fori_loop(1, req_count, arrived, 0)


def spread(queries, new_keys, new_values, cached_keys, cached_values, lengths, weight):
    requests, span, q_width = queries.shape
    slots, kv_width = cached_keys.shape[1:]
    key_heads = kv_width // HEAD_SIZE
    members = q_width // kv_width
    width = weight.shape[1]
    req_count, head_count = lax.axis_size("req"), lax.axis_size("head")
    chunks = 8
    blocks = req_count // chunks
    tile = blocks * 16
    lines = blocks * 8
    narrow = width // 2
    anywhere = pl.BlockSpec(memory_space=pl.ANY)
    dma = pltpu.SemaphoreType.DMA
    return pl.pallas_call(
        functools.partial(spread_kernel, (req_count, head_count, requests, key_heads, members)),
        in_specs=[pl.BlockSpec(memory_space=pltpu.SMEM)] + [anywhere] * 6,
        out_specs=anywhere,
        out_shape=jax.ShapeDtypeStruct((req_count * 8, width), BF16),
        scratch_shapes=[
            pltpu.VMEM((requests, blocks, span // blocks, q_width), BF16),
            pltpu.VMEM((requests, span, kv_width), BF16),
            pltpu.VMEM((requests, slots, kv_width), BF16),
            pltpu.VMEM((requests, key_heads, slots + span, 2 * HEAD_SIZE), BF16),
            pltpu.VMEM(weight.shape, BF16),
            pltpu.VMEM((q_width, narrow), BF16),
            pltpu.VMEM((requests, tile, q_width), F32),
            pltpu.VMEM((chunks, head_count, lines, q_width), BF16),
            pltpu.VMEM((chunks, head_count, lines, narrow), BF16),
            pltpu.VMEM((chunks, 2, lines, narrow // 2), BF16),
            pltpu.VMEM((chunks, 2, lines, narrow), BF16),
            pltpu.VMEM((chunks, 2, lines, q_width), BF16),
            pltpu.VMEM((4 * lines, 2 * q_width), BF16),
            pltpu.VMEM((chunks, 2, lines, narrow), BF16),
            pltpu.VMEM((chunks, lines, narrow), BF16),
            pltpu.VMEM((chunks, blocks, 8, width), BF16),
            dma((requests, 3 + 2 * key_heads)),
            dma,
            dma((2, 32)),
            dma((2, req_count)),
            dma((chunks, 2)),
            dma((chunks, 2)),
            dma((chunks,)),
            dma((chunks,)),
            dma((chunks, 2)),
            dma((chunks, 2)),
            dma((chunks, 2, 2)),
            dma((chunks, 2, 2)),
            dma((chunks, blocks)),
            dma((req_count,)),
            dma,
        ],
        compiler_params=pltpu.CompilerParams(
            collective_id=0, has_side_effects=True, vmem_limit_bytes=63 << 20
        ),
    )(
        lengths,
        queries.reshape(requests, blocks, span // blocks, q_width),
        new_keys,
        new_values,
        cached_keys,
        cached_values,
        weight,
    )


def norm_kernel(rows_ref, residual_ref, gain_ref, hidden_ref, normed_ref):
    count = rows_ref.shape[0]
    positions = residual_ref.shape[0]
    lines = residual_ref.shape[1]
    target = lax.broadcasted_iota(jnp.int32, (count, count), 0)
    source = lax.broadcasted_iota(jnp.int32, (count, count), 1)
    wanted = (target & (lines - 1)) * positions + (target >> (lines.bit_length() - 1))
    pick = (source == wanted).astype(F32).astype(BF16)
    moved = jnp.dot(pick, rows_ref[...], preferred_element_type=F32)
    summed = residual_ref[...].astype(F32) + moved.reshape(residual_ref.shape)
    hidden_ref[...] = summed.astype(BF16)
    mean_square = jnp.mean(summed * summed, axis=-1, keepdims=True)
    scale = lax.rsqrt(mean_square + 1e-05)
    normed_ref[...] = (summed * scale * gain_ref[...].astype(F32)[None, None]).astype(BF16)


def body(
    queries,
    new_keys,
    incoming_values,
    request_cached_keys,
    request_cached_values,
    cache_lengths,
    out_weight,
    residual,
    norm_gain,
):
    gathered = spread(
        queries,
        new_keys,
        incoming_values,
        request_cached_keys,
        request_cached_values,
        cache_lengths,
        out_weight,
    )
    positions, requests, width = residual.shape
    lines = 32
    block = pl.BlockSpec((positions, lines, width), lambda i: (0, i, 0))
    out = jax.ShapeDtypeStruct(residual.shape, BF16)
    hidden, normed = pl.pallas_call(
        norm_kernel,
        grid=(requests // lines,),
        in_specs=[
            pl.BlockSpec((positions * lines, width), lambda i: (i, 0)),
            block,
            pl.BlockSpec((width,), lambda i: (0,)),
        ],
        out_specs=[block, block],
        out_shape=[out, out],
        compiler_params=pltpu.CompilerParams(vmem_limit_bytes=63 << 20),
    )(gathered, residual, norm_gain)
    return hidden, normed


def solution(mesh):
    placed = (
        P("req", None, "head"),
        P("req", None, "head"),
        P("req", None, "head"),
        P("req", None, "head"),
        P("req", None, "head"),
        P("req"),
        P("head", None),
        P(("req", "head"), None, None),
        P(),
    )
    return jax.shard_map(
        body,
        mesh=mesh,
        in_specs=placed,
        out_specs=(P(("req", "head"), None, None), P(("req", "head"), None, None)),
        check_vma=False,
    )
```
